32 devices in a mesh: row: 4 (over z), col: 4 (over y, x), agent: 2 (over core).
Axes of the slice: x: 2, y: 2, z: 4, core: 2. Of those that a mesh axis runs over, the one named last changes fastest.
Arguments:
- raster: bfloat16 [2, 512, 512, 128], P(None, 'row', ('col', 'agent')), may hold values from -6 to 6
- first_kernel: bfloat16 [3, 3, 128, 128], replicated, may hold values from -0.1875 to 0.1875
- first_bias: float32 [128], replicated, may hold values from -3 to 3
- second_kernel: bfloat16 [3, 3, 128, 128], replicated, may hold values from -0.1875 to 0.1875
- second_bias: float32 [128], replicated, may hold values from -3 to 3
- queries: bfloat16 [256, 128], P('agent'), may hold values from -64 to 64
- agent_slot: int32 [256], replicated, may hold values from 0 to 255, each once
- regions: int32 [256, 4], replicated, may hold values from 0 to 8, as said below
Outputs:
- log_heatmap: float32 [2, 512, 512, 256], P(None, 'row', ('col', 'agent'))
The draws below stay inside these ranges and needn't reach their ends.
Inputs may be any that keep to these rules, and one draw needn't show every extreme that they name: regions[a,0] < regions[a,1] <= 8 and regions[a,2] < regions[a,3] <= 8.
All inputs are finite; a program needn't handle non-finite values.
Results may differ from the reference program's by a relative error of at most 0.0024.
Values may be sent and summed in bfloat16 or wider, within the bound.
A program may use at most 192 MiB of HBM per device.

```python
import jax
import jax.numpy as jnp

C = 128
A = 256
BLOCK = 64
SCENES = 2
H = 512
W = 512


def draw_queries(key, part):
    key_base = jax.random.fold_in(key, 11)
    key_pick = jax.random.fold_in(key, 14)
    key_jitter = jax.random.fold_in(key, 15)
    values = jnp.clip(0.4 * jax.random.normal(key_base, (A, C), jnp.float32), -1.6, 1.6)
    order = jax.random.permutation(key_pick, A)
    levels = jnp.zeros((A,), jnp.float32)
    levels = levels.at[order[0]].set(200.0 / C)
    levels = levels.at[order[1]].set(400.0 / C)
    levels = levels.at[order[2]].set(800.0 / C)
    jitter = 1.0 + 0.1 * jax.random.uniform(key_jitter, (A, C), jnp.float32, -1.0, 1.0)
    aligned = jnp.clip(levels[:, None] * jitter, -64.0, 64.0)
    values = jnp.where(levels[:, None] > 0.0, aligned, values)
    return values.astype(jnp.bfloat16)


def draw_regions(key, part):
    row_blocks = H // BLOCK
    col_blocks = W // BLOCK
    keys = [jax.random.fold_in(key, 21 + offset) for offset in range(4)]
    row_first = jax.random.randint(keys[0], (A,), 0, row_blocks // 2)
    row_end = row_first + jax.random.randint(keys[1], (A,), 1, row_blocks // 2 + 1)
    col_first = jax.random.randint(keys[2], (A,), 0, col_blocks // 2)
    col_end = col_first + jax.random.randint(keys[3], (A,), 1, col_blocks // 2 + 1)
    row_first = row_first.at[0].set(0)
    row_end = row_end.at[0].set(row_blocks)
    col_first = col_first.at[0].set(0)
    col_end = col_end.at[0].set(col_blocks)
    return jnp.stack([row_first, row_end, col_first, col_end], axis=1).astype(jnp.int32)


def level_of(stream_key, dims, pieces, smallest, largest):
    factor_of, own = 1.0, jax.random.fold_in(stream_key, 6)
    for dim, parts in pieces:
        steps = jnp.exp(jax.random.uniform(jax.random.fold_in(own, dim), (parts,), jnp.float32, smallest / len(pieces), largest / len(pieces)))
        factor_of = factor_of * jnp.repeat(steps, dims[dim] // parts).reshape([-1 if axis == dim else 1 for axis in range(len(dims))])
    return factor_of


def normal_values(stream_key, dims, spread, bound, split=(), held_as=jnp.bfloat16):
    drawn = spread * jax.random.normal(stream_key, dims, jnp.float32)
    if split:
        drawn = drawn * level_of(stream_key, dims, split, -0.22, 0.18)
    return jnp.clip(drawn, -bound, bound).astype(held_as)


def setup_inputs(seed: int = 0) -> dict:
    arg_keys = jax.random.split(jax.random.key(seed), 9)
    raster = normal_values(arg_keys[0], (SCENES, H, W, C), 1.0, 6.0, ((1, 4), (2, 8)))
    first_kernel = normal_values(arg_keys[1], (3, 3, C, C), (9 * C) ** -0.5, 0.1875)
    first_bias = normal_values(arg_keys[2], (C,), 0.5, 3.0, (), jnp.float32)
    second_kernel = normal_values(arg_keys[3], (3, 3, C, C), (9 * C) ** -0.5, 0.1875)
    second_bias = normal_values(arg_keys[4], (C,), 0.5, 3.0, (), jnp.float32)
    queries = draw_queries(jax.random.fold_in(arg_keys[8], 71), 0)
    agent_slot = jax.random.permutation(arg_keys[6], A).astype(jnp.int32)
    regions = draw_regions(jax.random.fold_in(arg_keys[8], 71), 0)
    return dict(raster=raster, first_kernel=first_kernel, first_bias=first_bias, second_kernel=second_kernel, second_bias=second_bias, queries=queries, agent_slot=agent_slot, regions=regions)


def dilated(image, kernel, bias, dilation):
    rows, cols, channels = image.shape
    padded = jnp.pad(image, ((dilation, dilation), (dilation, dilation), (0, 0)))
    running = jnp.zeros((rows * cols, kernel.shape[3]), jnp.float32)
    for row_tap in range(3):
        for col_tap in range(3):
            tap_piece = padded[row_tap * dilation:row_tap * dilation + rows, col_tap * dilation:col_tap * dilation + cols, :]
            running = running + jnp.dot(tap_piece.reshape(rows * cols, channels), kernel[row_tap, col_tap], preferred_element_type=jnp.float32)
    return jnp.maximum(running + bias, 0.0).astype(jnp.bfloat16).reshape(rows, cols, -1)


def reference(raster, first_kernel, first_bias, second_kernel, second_bias, queries, agent_slot, regions):
    ordered = queries[agent_slot]
    block_rows = jnp.arange(H, dtype=jnp.int32) // BLOCK
    block_cols = jnp.arange(W, dtype=jnp.int32) // BLOCK
    row_ok = (block_rows[:, None] >= regions[None, :, 0]) & (block_rows[:, None] < regions[None, :, 1])
    col_ok = (block_cols[:, None] >= regions[None, :, 2]) & (block_cols[:, None] < regions[None, :, 3])
    valid = row_ok[:, None, :] & col_ok[None, :, :]
    results = []
    for scene in range(SCENES):
        layer_one = dilated(raster[scene], first_kernel, first_bias, 4)
        layer_two = dilated(layer_one, second_kernel, second_bias, 8)
        logits = jnp.dot(layer_two.reshape(H * W, C), ordered.T, preferred_element_type=jnp.float32).reshape(H, W, A)
        masked = jnp.where(valid, logits, -1e30)
        peak = jnp.max(masked, axis=(0, 1))
        mass = jnp.sum(jnp.where(valid, jnp.exp(logits - peak), 0.0), axis=(0, 1))
        results.append(logits - (peak + jnp.log(mass)))
    return jnp.stack(results)
```

```python
import functools

import jax
import jax.numpy as jnp
from jax import lax
from jax.experimental import pallas as pl
from jax.experimental.pallas import tpu as pltpu
from jax.sharding import PartitionSpec as P

BLOCK = 64
PAD = 16
NEG = -1e30
SHARES = 4
MESH = pl.DeviceIdType.MESH
DIRS = ((-1, 0), (1, 0), (0, -1), (0, 1), (-1, -1), (-1, 1), (1, -1), (1, 1))
PIECES = DIRS + ((0, -1), (0, 1), (0, -1), (0, 1))
COUNTS = (10, 12)
TAPS = ((0, 2, -1), (1, 2, 1), (2, 1, -1), (1, 3, -1))
BF16 = jnp.bfloat16
F32 = jnp.float32


def field_kernel(
    nr, nc, na, scenes, rows, cols, agents,
    raster, w1, b1, w2, b2, queries, slot, regions,
    l2_out, keys_out, norm_out,
    xp1, q2, l2, z_ref, tops, sums, highs, p_edge, p_land, big1, big2, everyone, stats, w1_in, w2_in,
    load_sem, w_sem, out_sem, h_send, h_recv, k_send, k_recv, s_send, s_recv,
):
    r = lax.axis_index("row")
    c = lax.axis_index("col")
    a = lax.axis_index("agent")
    nq = nc * na
    n = nr * nq
    q = c * na + a
    pairs = rows // 2
    ch = w1.shape[-1]
    cut1 = pairs // 2 + 2
    half = rows // 2
    groups = cols // 16
    flat = groups + 1

    def place(rr, qq):
        return {"row": rr, "col": qq // na, "agent": qq % na}

    def exists(rr, qq):
        return (rr >= 0) & (rr < nr) & (qq >= 0) & (qq < nq)

    def others(fn):
        if n <= 32:
            rows_to = [(r + d) % nr for d in range(nr)]
            cols_to = [(q + d) % nq for d in range(nq)]
            for d in range(1, n):
                fn(d, rows_to[d // nq], cols_to[d % nq])
        else:
            pl.loop(1, n)(lambda d: fn(d, (r + d // nq) % nr, (q + d % nq) % nq))

    barrier = pltpu.get_barrier_semaphore()

    def greet(d, rr, qq):
        pl.semaphore_signal(barrier, inc=1, device_id=place(rr, qq), device_id_type=MESH)

    w_loads = [
        pltpu.make_async_copy(w1, w1_in, w_sem.at[0]),
        pltpu.make_async_copy(w2, w2_in, w_sem.at[1]),
    ]
    loads = [
        pltpu.make_async_copy(
            raster.at[s], xp1.at[s, pl.ds(2, pairs), :, pl.ds(PAD, cols), :], load_sem.at[s]
        )
        for s in range(scenes)
    ]
    loads[0].start()
    w_loads[0].start()
    others(greet)
    for load in loads[1:] + w_loads[1:]:
        load.start()

    def first_refs(s, d):
        dr, dq = PIECES[d]
        low, high = (cut1, pairs) if d >= 8 else (0, cut1)
        dst_k = {-1: pl.ds(pairs + 2, 2), 0: pl.ds(2 + low, high - low), 1: pl.ds(0, 2)}[dr]
        src_k = {-1: pl.ds(0, 2), 0: pl.ds(low, high - low), 1: pl.ds(pairs - 2, 2)}[dr]
        if dq == 0:
            return raster.at[s, src_k], xp1.at[s, dst_k, :, pl.ds(PAD, cols), :]
        side = 1 if dq == 1 else 0
        return p_edge.at[s, side, src_k], p_land.at[s, 1 - side, dst_k]

    def second_refs(s, d):
        dr, dq = PIECES[d]
        low, high = (half + 8, rows) if d >= 10 else (half, half + 8) if d >= 8 else (0, half)
        dst_r = {-1: pl.ds(rows + 8, 8), 0: pl.ds(8 + low, high - low), 1: pl.ds(0, 8)}[dr]
        src_r = {-1: pl.ds(8, 8), 0: pl.ds(8 + low, high - low), 1: pl.ds(rows, 8)}[dr]
        src_g = {-1: pl.ds(flat, 1), 0: pl.ds(1, 2 * groups), 1: pl.ds(groups, 1)}[dq]
        dst_g = {-1: pl.ds(2 * groups + 1, 1), 0: pl.ds(1, 2 * groups), 1: pl.ds(0, 1)}[dq]
        return q2.at[s, src_r, src_g], q2.at[s, dst_r, dst_g]

    def halo(phase, s, d):
        src, dst = (first_refs, second_refs)[phase](s, d)
        dr, dq = PIECES[d]
        return pltpu.make_async_remote_copy(
            src_ref=src, dst_ref=dst,
            send_sem=h_send.at[phase, s, d], recv_sem=h_recv.at[phase, s, d],
            device_id=place(r + dr, q + dq), device_id_type=MESH,
        )

    def start_halo(phase, s, picked):
        for d in picked:
            dr, dq = PIECES[d]

            @pl.when(exists(r + dr, q + dq))
            def _(d=d):
                halo(phase, s, d).start()

    def zero_halo(phase, s):
        for d in range(COUNTS[phase]):
            dr, dq = PIECES[d]

            @pl.when(jnp.logical_not(exists(r - dr, q - dq)))
            def _(d=d):
                dst = (first_refs, second_refs)[phase](s, d)[1]
                dst[...] = jnp.zeros(dst.shape, BF16)

    def recv_halo(phase, s, picked):
        for d in picked:
            dr, dq = PIECES[d]

            @pl.when(exists(r - dr, q - dq))
            def _(d=d):
                halo(phase, s, d).wait_recv()

    def sent_halo(phase, s):
        for d in range(COUNTS[phase]):
            dr, dq = PIECES[d]

            @pl.when(exists(r + dr, q + dq))
            def _(d=d):
                halo(phase, s, d).wait_send()

    def pack(s):
        @pl.loop(0, pairs // 8)
        def _(t):
            at = pl.ds(2 + t * 8, 8)
            to = pl.ds(t * 8, 8)
            for side, col in ((0, PAD), (1, PAD + cols - 4)):
                for par in range(2):
                    p_edge[s, side, to, 4 * par : 4 * par + 4, :] = xp1[s, at, par, col : col + 4, :]

    loads[0].wait()
    pack(0)
    pl.semaphore_wait(barrier, n - 1)
    start_halo(0, 0, (3, 2, 1, 6, 7, 9, 8, 0, 4, 5))

    here = queries.shape[0]

    def key_copy(d):
        other = (a + d) % na
        return pltpu.make_async_remote_copy(
            src_ref=queries, dst_ref=everyone.at[a],
            send_sem=k_send.at[d], recv_sem=k_recv.at[d],
            device_id=place(r, c * na + other), device_id_type=MESH,
        )

    for d in range(1, na):
        key_copy(d).start()
    everyone[a] = queries[...]

    for s in range(1, scenes):
        loads[s].wait()
        pack(s)
        start_halo(0, s, (3, 2, 1, 6, 7, 9, 8, 0, 4, 5))

    for phase in range(2):
        for s in range(scenes):
            zero_halo(phase, s)
    tops[...] = jnp.full(tops.shape, NEG, F32)
    sums[...] = jnp.zeros(sums.shape, F32)

    highs[...] = jnp.zeros(highs.shape, F32)

    @pl.loop(0, z_ref.shape[0] // 256)
    def _(t):
        z_ref[pl.ds(t * 256, 256)] = jnp.zeros((256, agents), F32)

    w_loads[0].wait()
    for i in range(4):
        for j in range(3):
            at = (i * 3 + j) * ch
            big1[at : at + ch, 0:ch] = w1_in[i, j] if i < 3 else jnp.zeros((ch, ch), BF16)
            big1[at : at + ch, ch : 2 * ch] = w1_in[i - 1, j] if i > 0 else jnp.zeros((ch, ch), BF16)

    w_loads[1].wait()
    for j in range(3):
        g0, g1, g2 = (w2_in[i, j].astype(F32) for i in range(3))
        mixed = (w2_in[0, j], (0.5 * (g0 + g1 + g2)).astype(BF16), (0.5 * (g0 - g1 + g2)).astype(BF16), w2_in[2, j])
        for i in range(4):
            for k in range(2):
                big2[i, (j + k) * ch : (j + k + 1) * ch, k * ch : (k + 1) * ch] = mixed[i]
    for i in range(4):
        for k in range(2):
            at = 3 * (1 - k)
            big2[i, at * ch : (at + 1) * ch, k * ch : (k + 1) * ch] = jnp.zeros((ch, ch), BF16)

    for d in range(1, na):
        key_copy(d).wait()
    table = everyone[...].reshape(na * here, ch)
    pick = (lax.broadcasted_iota(jnp.int32, (agents, agents), 0) == slot[...]).astype(F32).astype(BF16)
    keys = lax.dot_general(
        table, pick, (((0,), (0,)), ((), ())), preferred_element_type=F32
    ).astype(BF16)
    keys_out[...] = keys

    bias1 = jnp.concatenate([b1[...], b1[...]], axis=1)
    bias2 = jnp.concatenate([b2[...], b2[...]], axis=1)

    def layer_one(u):
        s, g = u // 2, u % 2

        def unpack():
            for t in range(0, pairs // 2 + 4, 4):
                at = pl.ds(g * (pairs // 2) + t, 4)
                for par in range(2):
                    for side, col in ((0, PAD - 4), (1, PAD + cols)):
                        xp1[s, at, par, col : col + 4, :] = (
                            p_land[s, side, at, 4 * par : 4 * par + 4, :]
                        )

        def body():
            def piece(i, j):
                parts = [
                    xp1[
                        s, pl.ds(g * half // 2 + 4 * h + 2 * i, 2), :,
                        PAD - 4 + 4 * j : PAD - 4 + 4 * j + cols, :,
                    ].reshape(4 * cols, ch)
                    for h in range(half // 8)
                ]
                return jnp.concatenate(parts, axis=0)

            lhs = jnp.concatenate([piece(i, j) for i in range(4) for j in range(3)], axis=1)
            out = jnp.dot(lhs, big1[...], preferred_element_type=F32)
            out = jnp.maximum(out + bias1, 0.0).astype(BF16)
            for h in range(half // 8):
                for o in range(2):
                    y = out[h * 4 * cols : (h + 1) * 4 * cols, o * ch : (o + 1) * ch]
                    y = y.reshape(4, groups, 2, 8, ch)
                    at = pl.ds(8 + half * g + 8 * h + 4 * o, 4)
                    q2[s, at, flat : flat + groups] = y[:, :, 0]
                    q2[s, at, 1 : 1 + groups] = y[:, :, 1]

        @pl.when(g == 0)
        def _():
            recv_halo(0, s, (1, 2, 3, 6, 7))

        @pl.when(g == 1)
        def _():
            recv_halo(0, s, (0, 4, 5, 8, 9))

        unpack()
        body()

        @pl.when(g == 0)
        def _():
            start_halo(1, s, (3, 2, 0, 4, 5))

        @pl.when(g == 1)
        def _():
            start_halo(1, s, (9, 8, 1, 6, 7, 11, 10))

    size = half * cols
    share = size // SHARES
    blocks = rows // BLOCK

    spare = scenes * blocks

    def fold(u, p):
        at = (u * half + p * (half // SHARES)) // BLOCK
        if not isinstance(u, int):
            at = jnp.where(u >= 0, at, spare)
        top, total = tops[at], sums[at]
        step = 64
        new = jnp.maximum(top, highs[p])
        total = total * jnp.exp(top - new)
        for k in range(share // step):
            low = p * share + k * step
            part = z_ref[low : low + step].reshape(step // 8, 8, agents)
            total = total + jnp.sum(jnp.exp(part - new[None]), axis=0)
        tops[at] = new
        sums[at] = total

    def layer_two(u):
        s, g = u // 2, u % 2

        @pl.when(g == 0)
        def _():
            recv_halo(1, s, (1, 2, 3, 6, 7, 8, 9))

        @pl.when(g == 1)
        def _():
            recv_halo(1, s, (0, 4, 5, 10, 11))

        def lhs(i):
            first, second, sign = TAPS[i]
            across = []
            for j in range(4):
                at = (j % 2) * flat + j // 2
                down = []
                for h in range(half // 16):
                    row = half * g + 16 * h
                    x = q2[s, pl.ds(row + 8 * first, 8), at : at + groups]
                    y = q2[s, pl.ds(row + 8 * second, 8), at : at + groups]
                    down.append((x + y if sign > 0 else x - y).reshape(8 * groups * 8, ch))
                across.append(jnp.concatenate(down, axis=0))
            return jnp.concatenate(across, axis=1)

        m = []
        for i in range(4):
            m.append(jnp.dot(lhs(i), big2[i], preferred_element_type=F32))
            for p in range(i * SHARES // 4, (i + 1) * SHARES // 4):
                fold(u - 1, p)
        outs = (
            jnp.maximum(m[0] + (m[1] + m[2]) + bias2, 0.0).astype(BF16),
            jnp.maximum((m[1] - m[2]) - m[3] + bias2, 0.0).astype(BF16),
        )
        for h in range(half // 16):
            for o in range(2):
                for k in range(2):
                    y = outs[o][h * 64 * groups : (h + 1) * 64 * groups, k * ch : (k + 1) * ch]
                    at = s * rows + half * g + 16 * h + 8 * o
                    l2[pl.ds(at, 8), :, k] = y.reshape(8, groups, 8, ch)
        for p in range(SHARES):
            deep = half // SHARES
            at = s * rows + half * g + p * deep
            y = l2[pl.ds(at, deep)].reshape(share, ch)
            z = jnp.dot(y, keys_out[...], preferred_element_type=F32)
            z_ref[p * share : (p + 1) * share] = z
            highs[p] = jnp.max(z.reshape(share // 8, 8, agents), axis=0)

        @pl.when((g == 0) & (s > 0))
        def _():
            share_stats(s - 1)

        @pl.when(g == 1)
        def _():
            out_copy(s).start()

    def settle(s):
        peak = jnp.full((1, agents), NEG, F32)
        mass = jnp.zeros((1, agents), F32)
        for block in range(blocks):
            top = tops[s * blocks + block]
            total = sums[s * blocks + block]
            high = jnp.max(top, axis=0, keepdims=True)
            part = jnp.sum(total * jnp.exp(top - high), axis=0, keepdims=True)
            block_row = r * blocks + block
            block_col = q * cols // BLOCK
            ok = (
                (regions[0:1] <= block_row) & (block_row < regions[1:2])
                & (regions[2:3] <= block_col) & (block_col < regions[3:4])
            )
            high = jnp.where(ok, high, NEG)
            part = jnp.where(ok, part, 0.0)
            new = jnp.maximum(peak, high)
            mass = mass * jnp.exp(peak - new) + part * jnp.exp(high - new)
            peak = new
        stats[s, 0, 0:1] = peak
        stats[s, 0, 1:2] = mass

    def stat_copy(s, d, rr, qq):
        return pltpu.make_async_remote_copy(
            src_ref=stats.at[s, 0], dst_ref=stats.at[s, d],
            send_sem=s_send.at[s, d], recv_sem=s_recv.at[s, d],
            device_id=place(rr, qq), device_id_type=MESH,
        )

    def share_stats(s):
        settle(s)
        others(lambda *to: stat_copy(s, *to).start())

    def finish(s):
        others(lambda *to: stat_copy(s, *to).wait_recv())
        peaks, parts = stats[s, :, 0, :], stats[s, :, 1, :]
        top = jnp.max(peaks, axis=0, keepdims=True)
        part = jnp.sum(parts * jnp.exp(peaks - top), axis=0, keepdims=True)
        norm_out[s : s + 1] = top + jnp.log(part)

    def out_copy(s):
        return pltpu.make_async_copy(l2.at[pl.ds(s * rows, rows)], l2_out.at[s], out_sem.at[s])

    pl.loop(0, 2 * scenes)(layer_one)
    pl.loop(0, 2 * scenes)(layer_two)
    for p in range(SHARES):
        fold(2 * scenes - 1, p)
    share_stats(scenes - 1)
    for phase in range(2):
        for s in range(scenes):
            sent_halo(phase, s)
    for s in range(scenes):
        finish(s)
    for s in range(scenes):
        others(lambda *to: stat_copy(s, *to).wait_send())
    for s in range(scenes):
        out_copy(s).wait()


def heat_kernel(field, keys, norm, out, cells, heat, in_sem, out_sem):
    scenes, total, _ = field.shape
    parts, size = cells.shape[0], cells.shape[1]
    slots = heat.shape[0]
    per = total // size
    loads = []
    for t in range(parts):
        load = pltpu.make_async_copy(
            field.at[t // per, pl.ds(t % per * size, size)], cells.at[t], in_sem.at[t]
        )
        load.start()
        loads.append(load)
    stores = []
    for t in range(parts):
        if t >= slots:
            stores[t - slots].wait()
        loads[t].wait()
        s = t // per
        heat[t % slots] = jnp.dot(cells[t], keys[...], preferred_element_type=F32) - norm[s : s + 1]
        store = pltpu.make_async_copy(
            heat.at[t % slots], out.at[s, pl.ds(t % per * size, size)], out_sem.at[t % slots]
        )
        store.start()
        stores.append(store)
    for store in stores[max(parts - slots, 0):]:
        store.wait()


def shards(nr, nc, na, raster, w1, b1, w2, b2, queries, slot, regions):
    scenes, rows, cols, ch = raster.shape
    agents = slot.shape[0]
    nq = nc * na
    vmem = pl.BlockSpec(memory_space=pltpu.VMEM)
    anywhere = pl.BlockSpec(memory_space=pl.ANY)
    dma = pltpu.SemaphoreType.DMA
    field, keys, norm = pl.pallas_call(
        functools.partial(field_kernel, nr, nc, na, scenes, rows, cols, agents),
        out_shape=(
            jax.ShapeDtypeStruct((scenes, rows, cols // 16, 2, 8, ch), BF16),
            jax.ShapeDtypeStruct((ch, agents), BF16),
            jax.ShapeDtypeStruct((scenes, agents), F32),
        ),
        in_specs=[anywhere, anywhere, vmem, anywhere, vmem, vmem, vmem, vmem],
        out_specs=(anywhere, vmem, vmem),
        scratch_shapes=[
            pltpu.VMEM((scenes, rows // 2 + 4, 2, cols + 2 * PAD, ch), BF16),
            pltpu.VMEM((scenes, rows + 16, 2 * (cols // 16 + 1), 8, ch), BF16),
            pltpu.VMEM((scenes * rows, cols // 16, 2, 8, ch), BF16),
            pltpu.VMEM((rows // 2 * cols, agents), F32),
            pltpu.VMEM((scenes * (rows // BLOCK) + 1, 8, agents), F32),
            pltpu.VMEM((scenes * (rows // BLOCK) + 1, 8, agents), F32),
            pltpu.VMEM((SHARES, 8, agents), F32),
            pltpu.VMEM((scenes, 2, rows // 2, 8, ch), BF16),
            pltpu.VMEM((scenes, 2, rows // 2 + 4, 8, ch), BF16),
            pltpu.VMEM((12 * ch, 2 * ch), BF16),
            pltpu.VMEM((4, 4 * ch, 2 * ch), BF16),
            pltpu.VMEM((na,) + queries.shape, BF16),
            pltpu.VMEM((scenes, nr * nq, 2, agents), F32),
            pltpu.VMEM(w1.shape, BF16),
            pltpu.VMEM(w2.shape, BF16),
            dma((scenes,)),
            dma((2,)),
            dma((scenes,)),
            dma((2, scenes, 12)),
            dma((2, scenes, 12)),
            dma((na,)),
            dma((na,)),
            dma((scenes, nr * nq)),
            dma((scenes, nr * nq)),
        ],
        compiler_params=pltpu.CompilerParams(
            collective_id=0, has_side_effects=True, vmem_limit_bytes=60 * 1024 * 1024
        ),
        name="field",
    )(
        raster.reshape(scenes, rows // 2, 2, cols, ch), w1, b1.reshape(1, -1), w2, b2.reshape(1, -1),
        queries, slot.reshape(1, -1), regions.T,
    )
    cells = rows * cols
    size = min(2048, cells)
    parts = scenes * cells // size
    slots = min(4, parts)
    heat = pl.pallas_call(
        heat_kernel,
        out_shape=jax.ShapeDtypeStruct((scenes, cells, agents), F32),
        in_specs=[anywhere, vmem, vmem],
        out_specs=anywhere,
        scratch_shapes=[
            pltpu.VMEM((parts, size, ch), BF16),
            pltpu.VMEM((slots, size, agents), F32),
            dma((parts,)),
            dma((slots,)),
        ],
        name="heat",
    )(field.reshape(scenes, cells, ch), keys, norm)
    return heat.reshape(scenes, rows, cols, agents)


def solution(mesh):
    in_specs = (P(None, "row", ("col", "agent"), None), P(), P(), P(), P(), P("agent", None), P(), P())
    out_specs = P(None, "row", ("col", "agent"), None)
    sizes = (mesh.shape["row"], mesh.shape["col"], mesh.shape["agent"])
    return jax.shard_map(
        functools.partial(shards, *sizes), mesh=mesh, in_specs=in_specs, out_specs=out_specs, check_vma=False
    )
```

```python
import functools

import jax
import jax.numpy as jnp
from jax import lax
from jax.experimental import pallas as pl
from jax.experimental.pallas import tpu as pltpu
from jax.sharding import PartitionSpec as P

BLOCK = 64
PAD = 16
NEG = -1e30
SHARES = 4
MESH = pl.DeviceIdType.MESH
DIRS = ((-1, 0), (1, 0), (0, -1), (0, 1), (-1, -1), (-1, 1), (1, -1), (1, 1))
PIECES = DIRS + ((0, -1), (0, 1), (0, -1), (0, 1))
COUNTS = (10, 12)
TAPS = ((0, 2, -1), (1, 2, 1), (2, 1, -1), (1, 3, -1))
BF16 = jnp.bfloat16
F32 = jnp.float32


def field_kernel(
    nr, nc, na, scenes, rows, cols, agents,
    raster, w1, b1, w2, b2, queries, slot, regions,
    l2_out, keys_out, norm_out,
    xp1, q2, l2, z_ref, tops, sums, highs, p_edge, p_land, big1, big2, everyone, stats, w1_in, w2_in,
    load_sem, w_sem, out_sem, h_send, h_recv, k_send, k_recv, s_send, s_recv,
):
    r = lax.axis_index("row")
    c = lax.axis_index("col")
    a = lax.axis_index("agent")
    nq = nc * na
    n = nr * nq
    q = c * na + a
    pairs = rows // 2
    ch = w1.shape[-1]
    cut1 = pairs // 2 + 2
    half = rows // 2
    groups = cols // 16
    flat = groups + 1

    def place(rr, qq):
        return {"row": rr, "col": qq // na, "agent": qq % na}

    def exists(rr, qq):
        return (rr >= 0) & (rr < nr) & (qq >= 0) & (qq < nq)

    def others(fn):
        if n <= 32:
            rows_to = [(r + d) % nr for d in range(nr)]
            cols_to = [(q + d) % nq for d in range(nq)]
            for d in range(1, n):
                fn(d, rows_to[d // nq], cols_to[d % nq])
        else:
            pl.loop(1, n)(lambda d: fn(d, (r + d // nq) % nr, (q + d % nq) % nq))

    barrier = pltpu.get_barrier_semaphore()

    def greet(d, rr, qq):
        pl.semaphore_signal(barrier, inc=1, device_id=place(rr, qq), device_id_type=MESH)

    w_loads = [
        pltpu.make_async_copy(w1, w1_in, w_sem.at[0]),
        pltpu.make_async_copy(w2, w2_in, w_sem.at[1]),
    ]
    loads = [
        pltpu.make_async_copy(
            raster.at[s], xp1.at[s, pl.ds(2, pairs), :, pl.ds(PAD, cols), :], load_sem.at[s]
        )
        for s in range(scenes)
    ]
    loads[0].start()
    w_loads[0].start()
    others(greet)
    for load in loads[1:] + w_loads[1:]:
        load.start()

    def first_refs(s, d):
        dr, dq = PIECES[d]
        low, high = (cut1, pairs) if d >= 8 else (0, cut1)
        dst_k = {-1: pl.ds(pairs + 2, 2), 0: pl.ds(2 + low, high - low), 1: pl.ds(0, 2)}[dr]
        src_k = {-1: pl.ds(0, 2), 0: pl.ds(low, high - low), 1: pl.ds(pairs - 2, 2)}[dr]
        if dq == 0:
            return raster.at[s, src_k], xp1.at[s, dst_k, :, pl.ds(PAD, cols), :]
        side = 1 if dq == 1 else 0
        return p_edge.at[s, side, src_k], p_land.at[s, 1 - side, dst_k]

    def second_refs(s, d):
        dr, dq = PIECES[d]
        low, high = (half + 8, rows) if d >= 10 else (half, half + 8) if d >= 8 else (0, half)
        dst_r = {-1: pl.ds(rows + 8, 8), 0: pl.ds(8 + low, high - low), 1: pl.ds(0, 8)}[dr]
        src_r = {-1: pl.ds(8, 8), 0: pl.ds(8 + low, high - low), 1: pl.ds(rows, 8)}[dr]
        src_g = {-1: pl.ds(flat, 1), 0: pl.ds(1, 2 * groups), 1: pl.ds(groups, 1)}[dq]
        dst_g = {-1: pl.ds(2 * groups + 1, 1), 0: pl.ds(1, 2 * groups), 1: pl.ds(0, 1)}[dq]
        return q2.at[s, src_r, src_g], q2.at[s, dst_r, dst_g]

    def halo(phase, s, d):
        src, dst = (first_refs, second_refs)[phase](s, d)
        dr, dq = PIECES[d]
        return pltpu.make_async_remote_copy(
            src_ref=src, dst_ref=dst,
            send_sem=h_send.at[phase, s, d], recv_sem=h_recv.at[phase, s, d],
            device_id=place(r + dr, q + dq), device_id_type=MESH,
        )

    def start_halo(phase, s, picked):
        for d in picked:
            dr, dq = PIECES[d]

            @pl.when(exists(r + dr, q + dq))
            def _(d=d):
                halo(phase, s, d).start()

    def zero_halo(phase, s):
        for d in range(COUNTS[phase]):
            dr, dq = PIECES[d]

            @pl.when(jnp.logical_not(exists(r - dr, q - dq)))
            def _(d=d):
                dst = (first_refs, second_refs)[phase](s, d)[1]
                dst[...] = jnp.zeros(dst.shape, BF16)

    def recv_halo(phase, s, picked):
        for d in picked:
            dr, dq = PIECES[d]

            @pl.when(exists(r - dr, q - dq))
            def _(d=d):
                halo(phase, s, d).wait_recv()

    def sent_halo(phase, s):
        for d in range(COUNTS[phase]):
            dr, dq = PIECES[d]

            @pl.when(exists(r + dr, q + dq))
            def _(d=d):
                halo(phase, s, d).wait_send()

    def pack(s):
        @pl.loop(0, pairs // 8)
        def _(t):
            at = pl.ds(2 + t * 8, 8)
            to = pl.ds(t * 8, 8)
            for side, col in ((0, PAD), (1, PAD + cols - 4)):
                for par in range(2):
                    p_edge[s, side, to, 4 * par : 4 * par + 4, :] = xp1[s, at, par, col : col + 4, :]

    loads[0].wait()
    pack(0)
    pl.semaphore_wait(barrier, n - 1)
    start_halo(0, 0, (6, 7, 3, 2, 1, 4, 5, 9, 8, 0))

    here = queries.shape[0]

    def key_copy(d):
        other = (a + d) % na
        return pltpu.make_async_remote_copy(
            src_ref=queries, dst_ref=everyone.at[a],
            send_sem=k_send.at[d], recv_sem=k_recv.at[d],
            device_id=place(r, c * na + other), device_id_type=MESH,
        )

    for d in range(1, na):
        key_copy(d).start()
    everyone[a] = queries[...]

    for s in range(1, scenes):
        loads[s].wait()
        pack(s)
        start_halo(0, s, (6, 7, 3, 2, 1, 4, 5, 9, 8, 0))

    for phase in range(2):
        for s in range(scenes):
            zero_halo(phase, s)
    tops[...] = jnp.full(tops.shape, NEG, F32)
    sums[...] = jnp.zeros(sums.shape, F32)

    highs[...] = jnp.zeros(highs.shape, F32)

    @pl.loop(0, z_ref.shape[0] // 256)
    def _(t):
        z_ref[pl.ds(t * 256, 256)] = jnp.zeros((256, agents), F32)

    w_loads[0].wait()
    for i in range(4):
        for j in range(3):
            at = (i * 3 + j) * ch
            big1[at : at + ch, 0:ch] = w1_in[i, j] if i < 3 else jnp.zeros((ch, ch), BF16)
            big1[at : at + ch, ch : 2 * ch] = w1_in[i - 1, j] if i > 0 else jnp.zeros((ch, ch), BF16)

    w_loads[1].wait()
    for j in range(3):
        g0, g1, g2 = (w2_in[i, j].astype(F32) for i in range(3))
        mixed = (w2_in[0, j], (0.5 * (g0 + g1 + g2)).astype(BF16), (0.5 * (g0 - g1 + g2)).astype(BF16), w2_in[2, j])
        for i in range(4):
            for k in range(2):
                big2[i, (j + k) * ch : (j + k + 1) * ch, k * ch : (k + 1) * ch] = mixed[i]
    for i in range(4):
        for k in range(2):
            at = 3 * (1 - k)
            big2[i, at * ch : (at + 1) * ch, k * ch : (k + 1) * ch] = jnp.zeros((ch, ch), BF16)

    for d in range(1, na):
        key_copy(d).wait()
    table = everyone[...].reshape(na * here, ch)
    pick = (lax.broadcasted_iota(jnp.int32, (agents, agents), 0) == slot[...]).astype(F32).astype(BF16)
    keys = lax.dot_general(
        table, pick, (((0,), (0,)), ((), ())), preferred_element_type=F32
    ).astype(BF16)
    keys_out[...] = keys

    bias1 = jnp.concatenate([b1[...], b1[...]], axis=1)
    bias2 = jnp.concatenate([b2[...], b2[...]], axis=1)

    def layer_one(u):
        s, g = u // 2, u % 2

        def unpack():
            for t in range(0, pairs // 2 + 4, 4):
                at = pl.ds(g * (pairs // 2) + t, 4)
                for par in range(2):
                    for side, col in ((0, PAD - 4), (1, PAD + cols)):
                        xp1[s, at, par, col : col + 4, :] = (
                            p_land[s, side, at, 4 * par : 4 * par + 4, :]
                        )

        def body():
            def piece(i, j):
                parts = [
                    xp1[
                        s, pl.ds(g * half // 2 + 4 * h + 2 * i, 2), :,
                        PAD - 4 + 4 * j : PAD - 4 + 4 * j + cols, :,
                    ].reshape(4 * cols, ch)
                    for h in range(half // 8)
                ]
                return jnp.concatenate(parts, axis=0)

            lhs = jnp.concatenate([piece(i, j) for i in range(4) for j in range(3)], axis=1)
            out = jnp.dot(lhs, big1[...], preferred_element_type=F32)
            out = jnp.maximum(out + bias1, 0.0).astype(BF16)
            for h in range(half // 8):
                for o in range(2):
                    y = out[h * 4 * cols : (h + 1) * 4 * cols, o * ch : (o + 1) * ch]
                    y = y.reshape(4, groups, 2, 8, ch)
                    at = pl.ds(8 + half * g + 8 * h + 4 * o, 4)
                    q2[s, at, flat : flat + groups] = y[:, :, 0]
                    q2[s, at, 1 : 1 + groups] = y[:, :, 1]

        @pl.when(g == 0)
        def _():
            recv_halo(0, s, (1, 2, 3, 6, 7))

        @pl.when(g == 1)
        def _():
            recv_halo(0, s, (0, 4, 5, 8, 9))

        unpack()
        body()

        @pl.when(g == 0)
        def _():
            start_halo(1, s, (4, 5, 3, 2, 0))

        @pl.when(g == 1)
        def _():
            start_halo(1, s, (6, 7, 9, 8, 1, 11, 10))

    size = half * cols
    share = size // SHARES
    blocks = rows // BLOCK

    spare = scenes * blocks

    def fold(u, p):
        at = (u * half + p * (half // SHARES)) // BLOCK
        if not isinstance(u, int):
            at = jnp.where(u >= 0, at, spare)
        top, total = tops[at], sums[at]
        step = 64
        new = jnp.maximum(top, highs[p])
        total = total * jnp.exp(top - new)
        for k in range(share // step):
            low = p * share + k * step
            part = z_ref[low : low + step].reshape(step // 8, 8, agents)
            total = total + jnp.sum(jnp.exp(part - new[None]), axis=0)
        tops[at] = new
        sums[at] = total

    def layer_two(u):
        s, g = u // 2, u % 2

        @pl.when(g == 0)
        def _():
            recv_halo(1, s, (1, 2, 3, 6, 7, 8, 9))

        @pl.when(g == 1)
        def _():
            recv_halo(1, s, (0, 4, 5, 10, 11))

        def lhs(i):
            first, second, sign = TAPS[i]
            across = []
            for j in range(4):
                at = (j % 2) * flat + j // 2
                down = []
                for h in range(half // 16):
                    row = half * g + 16 * h
                    x = q2[s, pl.ds(row + 8 * first, 8), at : at + groups]
                    y = q2[s, pl.ds(row + 8 * second, 8), at : at + groups]
                    down.append((x + y if sign > 0 else x - y).reshape(8 * groups * 8, ch))
                across.append(jnp.concatenate(down, axis=0))
            return jnp.concatenate(across, axis=1)

        m = []
        for i in range(4):
            m.append(jnp.dot(lhs(i), big2[i], preferred_element_type=F32))
            for p in range(i * SHARES // 4, (i + 1) * SHARES // 4):
                fold(u - 1, p)
        outs = (
            jnp.maximum(m[0] + (m[1] + m[2]) + bias2, 0.0).astype(BF16),
            jnp.maximum((m[1] - m[2]) - m[3] + bias2, 0.0).astype(BF16),
        )
        for h in range(half // 16):
            for o in range(2):
                for k in range(2):
                    y = outs[o][h * 64 * groups : (h + 1) * 64 * groups, k * ch : (k + 1) * ch]
                    at = s * rows + half * g + 16 * h + 8 * o
                    l2[pl.ds(at, 8), :, k] = y.reshape(8, groups, 8, ch)
        for p in range(SHARES):
            deep = half // SHARES
            at = s * rows + half * g + p * deep
            y = l2[pl.ds(at, deep)].reshape(share, ch)
            z = jnp.dot(y, keys_out[...], preferred_element_type=F32)
            z_ref[p * share : (p + 1) * share] = z
            highs[p] = jnp.max(z.reshape(share // 8, 8, agents), axis=0)

        @pl.when(g == 1)
        def _():
            out_copy(s).start()

    def settle(s):
        peak = jnp.full((1, agents), NEG, F32)
        mass = jnp.zeros((1, agents), F32)
        for block in range(blocks):
            top = tops[s * blocks + block]
            total = sums[s * blocks + block]
            high = jnp.max(top, axis=0, keepdims=True)
            part = jnp.sum(total * jnp.exp(top - high), axis=0, keepdims=True)
            block_row = r * blocks + block
            block_col = q * cols // BLOCK
            ok = (
                (regions[0:1] <= block_row) & (block_row < regions[1:2])
                & (regions[2:3] <= block_col) & (block_col < regions[3:4])
            )
            high = jnp.where(ok, high, NEG)
            part = jnp.where(ok, part, 0.0)
            new = jnp.maximum(peak, high)
            mass = mass * jnp.exp(peak - new) + part * jnp.exp(high - new)
            peak = new
        stats[0, 0, s : s + 1] = peak
        stats[0, 1, s : s + 1] = mass

    def stat_copy(d, rr, qq):
        return pltpu.make_async_remote_copy(
            src_ref=stats.at[0], dst_ref=stats.at[d],
            send_sem=s_send.at[d], recv_sem=s_recv.at[d],
            device_id=place(rr, qq), device_id_type=MESH,
        )

    def out_copy(s):
        return pltpu.make_async_copy(l2.at[pl.ds(s * rows, rows)], l2_out.at[s], out_sem.at[s])

    pl.loop(0, 2 * scenes)(layer_one)
    pl.loop(0, 2 * scenes)(layer_two)
    for p in range(SHARES):
        fold(2 * scenes - 1, p)
    for s in range(scenes):
        settle(s)
    others(lambda *to: stat_copy(*to).start())
    for phase in range(2):
        for s in range(scenes):
            sent_halo(phase, s)
    others(lambda *to: stat_copy(*to).wait_recv())
    peaks, parts = stats[:, 0], stats[:, 1]
    top = jnp.max(peaks, axis=0)
    part = jnp.sum(parts * jnp.exp(peaks - top[None]), axis=0)
    norm_out[...] = top + jnp.log(part)
    others(lambda *to: stat_copy(*to).wait_send())
    for s in range(scenes):
        out_copy(s).wait()


def heat_kernel(field, keys, norm, out, cells, heat, in_sem, out_sem):
    scenes, total, _ = field.shape
    slots, size = heat.shape[0], heat.shape[1]
    batch = cells.shape[1]
    parts = scenes * total // size
    per = total // size
    many = batch // size

    def load(t):
        return pltpu.make_async_copy(
            field.at[t * batch // total, pl.ds(t * batch % total, batch)], cells.at[t], in_sem.at[t]
        )

    def store(t):
        return pltpu.make_async_copy(
            heat.at[t % slots], out.at[t // per, pl.ds(t % per * size, size)], out_sem.at[t % slots]
        )

    for t in range(cells.shape[0]):
        load(t).start()

    @pl.loop(0, parts)
    def _(t):
        @pl.when(t % many == 0)
        def _():
            load(t // many).wait()

        @pl.when(t >= slots)
        def _():
            store(t - slots).wait()

        y = cells[t // many, pl.ds(t % many * size, size)]
        z = jnp.dot(y, keys[...], preferred_element_type=F32)
        heat[t % slots] = z - norm[pl.ds(t // per, 1)]
        store(t).start()

    for t in range(parts - slots, parts):
        store(t).wait()


def shards(nr, nc, na, raster, w1, b1, w2, b2, queries, slot, regions):
    scenes, rows, cols, ch = raster.shape
    agents = slot.shape[0]
    nq = nc * na
    vmem = pl.BlockSpec(memory_space=pltpu.VMEM)
    anywhere = pl.BlockSpec(memory_space=pl.ANY)
    dma = pltpu.SemaphoreType.DMA
    field, keys, norm = pl.pallas_call(
        functools.partial(field_kernel, nr, nc, na, scenes, rows, cols, agents),
        out_shape=(
            jax.ShapeDtypeStruct((scenes, rows, cols // 16, 2, 8, ch), BF16),
            jax.ShapeDtypeStruct((ch, agents), BF16),
            jax.ShapeDtypeStruct((scenes, agents), F32),
        ),
        in_specs=[anywhere, anywhere, vmem, anywhere, vmem, vmem, vmem, vmem],
        out_specs=(anywhere, vmem, vmem),
        scratch_shapes=[
            pltpu.VMEM((scenes, rows // 2 + 4, 2, cols + 2 * PAD, ch), BF16),
            pltpu.VMEM((scenes, rows + 16, 2 * (cols // 16 + 1), 8, ch), BF16),
            pltpu.VMEM((scenes * rows, cols // 16, 2, 8, ch), BF16),
            pltpu.VMEM((rows // 2 * cols, agents), F32),
            pltpu.VMEM((scenes * (rows // BLOCK) + 1, 8, agents), F32),
            pltpu.VMEM((scenes * (rows // BLOCK) + 1, 8, agents), F32),
            pltpu.VMEM((SHARES, 8, agents), F32),
            pltpu.VMEM((scenes, 2, rows // 2, 8, ch), BF16),
            pltpu.VMEM((scenes, 2, rows // 2 + 4, 8, ch), BF16),
            pltpu.VMEM((12 * ch, 2 * ch), BF16),
            pltpu.VMEM((4, 4 * ch, 2 * ch), BF16),
            pltpu.VMEM((na,) + queries.shape, BF16),
            pltpu.VMEM((nr * nq, 2, scenes, agents), F32),
            pltpu.VMEM(w1.shape, BF16),
            pltpu.VMEM(w2.shape, BF16),
            dma((scenes,)),
            dma((2,)),
            dma((scenes,)),
            dma((2, scenes, 12)),
            dma((2, scenes, 12)),
            dma((na,)),
            dma((na,)),
            dma((nr * nq,)),
            dma((nr * nq,)),
        ],
        compiler_params=pltpu.CompilerParams(
            collective_id=0, has_side_effects=True, vmem_limit_bytes=60 * 1024 * 1024
        ),
        name="field",
    )(
        raster.reshape(scenes, rows // 2, 2, cols, ch), w1, b1.reshape(1, -1), w2, b2.reshape(1, -1),
        queries, slot.reshape(1, -1), regions.T,
    )
    cells = rows * cols
    size = min(1024, cells)
    batch = min(2048, cells)
    parts = scenes * cells // size
    slots = min(8, parts)
    heat = pl.pallas_call(
        heat_kernel,
        out_shape=jax.ShapeDtypeStruct((scenes, cells, agents), F32),
        in_specs=[anywhere, vmem, vmem],
        out_specs=anywhere,
        scratch_shapes=[
            pltpu.VMEM((scenes * cells // batch, batch, ch), BF16),
            pltpu.VMEM((slots, size, agents), F32),
            dma((scenes * cells // batch,)),
            dma((slots,)),
        ],
        name="heat",
    )(field.reshape(scenes, cells, ch), keys, norm)
    return heat.reshape(scenes, rows, cols, agents)


def solution(mesh):
    in_specs = (P(None, "row", ("col", "agent"), None), P(), P(), P(), P(), P("agent", None), P(), P())
    out_specs = P(None, "row", ("col", "agent"), None)
    sizes = (mesh.shape["row"], mesh.shape["col"], mesh.shape["agent"])
    return jax.shard_map(
        functools.partial(shards, *sizes), mesh=mesh, in_specs=in_specs, out_specs=out_specs, check_vma=False
    )
```

```python
import functools

import jax
import jax.numpy as jnp
from jax import lax
from jax.experimental import pallas as pl
from jax.experimental.pallas import tpu as pltpu
from jax.sharding import PartitionSpec as P

BLOCK = 64
PAD = 16
NEG = -1e30
SHARES = 4
MESH = pl.DeviceIdType.MESH
DIRS = ((-1, 0), (1, 0), (0, -1), (0, 1), (-1, -1), (-1, 1), (1, -1), (1, 1))
PIECES = DIRS + ((0, -1), (0, 1), (0, -1), (0, 1))
COUNTS = (10, 12)
TAPS = ((0, 2, -1), (1, 2, 1), (2, 1, -1), (1, 3, -1))
BF16 = jnp.bfloat16
F32 = jnp.float32


def field_kernel(
    nr, nc, na, scenes, rows, cols, agents,
    raster, w1, b1, w2, b2, queries, slot, regions,
    l2_out, keys_out, norm_out,
    xp1, q2, l2, z_ref, tops, sums, highs, p_edge, p_land, big1, big2, everyone, stats, w1_in, w2_in,
    load_sem, w_sem, out_sem, h_send, h_recv, k_send, k_recv, s_send, s_recv,
):
    r = lax.axis_index("row")
    c = lax.axis_index("col")
    a = lax.axis_index("agent")
    nq = nc * na
    n = nr * nq
    q = c * na + a
    pairs = rows // 2
    ch = w1.shape[-1]
    cut1 = pairs // 2 + 2
    half = rows // 2
    groups = cols // 16
    flat = groups + 1

    def place(rr, qq):
        return {"row": rr, "col": qq // na, "agent": qq % na}

    def exists(rr, qq):
        return (rr >= 0) & (rr < nr) & (qq >= 0) & (qq < nq)

    def others(fn):
        if n <= 32:
            rows_to = [(r + d) % nr for d in range(nr)]
            cols_to = [(q + d) % nq for d in range(nq)]
            for d in range(1, n):
                fn(d, rows_to[d // nq], cols_to[d % nq])
        else:
            pl.loop(1, n)(lambda d: fn(d, (r + d // nq) % nr, (q + d % nq) % nq))

    barrier = pltpu.get_barrier_semaphore()

    def greet(d, rr, qq):
        pl.semaphore_signal(barrier, inc=1, device_id=place(rr, qq), device_id_type=MESH)

    w_loads = [
        pltpu.make_async_copy(w1, w1_in, w_sem.at[0]),
        pltpu.make_async_copy(w2, w2_in, w_sem.at[1]),
    ]
    loads = [
        pltpu.make_async_copy(
            raster.at[s], xp1.at[s, pl.ds(2, pairs), :, pl.ds(PAD, cols), :], load_sem.at[s]
        )
        for s in range(scenes)
    ]
    loads[0].start()
    others(greet)
    w_loads[0].start()
    for load in loads[1:] + w_loads[1:]:
        load.start()

    def first_refs(s, d):
        dr, dq = PIECES[d]
        low, high = (cut1, pairs) if d >= 8 else (0, cut1)
        dst_k = {-1: pl.ds(pairs + 2, 2), 0: pl.ds(2 + low, high - low), 1: pl.ds(0, 2)}[dr]
        src_k = {-1: pl.ds(0, 2), 0: pl.ds(low, high - low), 1: pl.ds(pairs - 2, 2)}[dr]
        if dq == 0:
            return raster.at[s, src_k], xp1.at[s, dst_k, :, pl.ds(PAD, cols), :]
        side = 1 if dq == 1 else 0
        return p_edge.at[s, side, src_k], p_land.at[s, 1 - side, dst_k]

    def second_refs(s, d):
        dr, dq = PIECES[d]
        low, high = (half + 8, rows) if d >= 10 else (half, half + 8) if d >= 8 else (0, half)
        dst_r = {-1: pl.ds(rows + 8, 8), 0: pl.ds(8 + low, high - low), 1: pl.ds(0, 8)}[dr]
        src_r = {-1: pl.ds(8, 8), 0: pl.ds(8 + low, high - low), 1: pl.ds(rows, 8)}[dr]
        src_g = {-1: pl.ds(flat, 1), 0: pl.ds(1, 2 * groups), 1: pl.ds(groups, 1)}[dq]
        dst_g = {-1: pl.ds(2 * groups + 1, 1), 0: pl.ds(1, 2 * groups), 1: pl.ds(0, 1)}[dq]
        return q2.at[s, src_r, src_g], q2.at[s, dst_r, dst_g]

    def halo(phase, s, d):
        src, dst = (first_refs, second_refs)[phase](s, d)
        dr, dq = PIECES[d]
        return pltpu.make_async_remote_copy(
            src_ref=src, dst_ref=dst,
            send_sem=h_send.at[phase, s, d], recv_sem=h_recv.at[phase, s, d],
            device_id=place(r + dr, q + dq), device_id_type=MESH,
        )

    def start_halo(phase, s, picked):
        for d in picked:
            dr, dq = PIECES[d]

            @pl.when(exists(r + dr, q + dq))
            def _(d=d):
                halo(phase, s, d).start()

    def zero_halo(phase, s):
        for d in range(COUNTS[phase]):
            dr, dq = PIECES[d]

            @pl.when(jnp.logical_not(exists(r - dr, q - dq)))
            def _(d=d):
                dst = (first_refs, second_refs)[phase](s, d)[1]
                dst[...] = jnp.zeros(dst.shape, BF16)

    def recv_halo(phase, s, picked):
        for d in picked:
            dr, dq = PIECES[d]

            @pl.when(exists(r - dr, q - dq))
            def _(d=d):
                halo(phase, s, d).wait_recv()

    def sent_halo(phase, s):
        for d in range(COUNTS[phase]):
            dr, dq = PIECES[d]

            @pl.when(exists(r + dr, q + dq))
            def _(d=d):
                halo(phase, s, d).wait_send()

    def pack(s):
        @pl.loop(0, pairs // 8)
        def _(t):
            at = pl.ds(2 + t * 8, 8)
            to = pl.ds(t * 8, 8)
            for side, col in ((0, PAD), (1, PAD + cols - 4)):
                for par in range(2):
                    p_edge[s, side, to, 4 * par : 4 * par + 4, :] = xp1[s, at, par, col : col + 4, :]

    loads[0].wait()
    pack(0)
    pl.semaphore_wait(barrier, n - 1)
    start_halo(0, 0, (6, 7, 1, 3, 2, 4, 5, 0, 9, 8))
    for s in range(1, scenes):
        start_halo(0, s, (1, 0))

    here = queries.shape[0]

    def key_copy(d):
        other = (a + d) % na
        return pltpu.make_async_remote_copy(
            src_ref=queries, dst_ref=everyone.at[a],
            send_sem=k_send.at[d], recv_sem=k_recv.at[d],
            device_id=place(r, c * na + other), device_id_type=MESH,
        )

    for d in range(1, na):
        key_copy(d).start()
    everyone[a] = queries[...]

    for s in range(1, scenes):
        loads[s].wait()
        pack(s)
        start_halo(0, s, (6, 7, 3, 2, 4, 5, 9, 8))

    for phase in range(2):
        for s in range(scenes):
            zero_halo(phase, s)
    tops[...] = jnp.full(tops.shape, NEG, F32)
    sums[...] = jnp.zeros(sums.shape, F32)

    highs[...] = jnp.zeros(highs.shape, F32)

    @pl.loop(0, z_ref.shape[0] // 256)
    def _(t):
        z_ref[pl.ds(t * 256, 256)] = jnp.zeros((256, agents), F32)

    w_loads[0].wait()
    for i in range(4):
        for j in range(3):
            at = (i * 3 + j) * ch
            big1[at : at + ch, 0:ch] = w1_in[i, j] if i < 3 else jnp.zeros((ch, ch), BF16)
            big1[at : at + ch, ch : 2 * ch] = w1_in[i - 1, j] if i > 0 else jnp.zeros((ch, ch), BF16)

    w_loads[1].wait()
    for j in range(3):
        g0, g1, g2 = (w2_in[i, j].astype(F32) for i in range(3))
        mixed = (w2_in[0, j], (0.5 * (g0 + g1 + g2)).astype(BF16), (0.5 * (g0 - g1 + g2)).astype(BF16), w2_in[2, j])
        for i in range(4):
            for k in range(2):
                big2[i, (j + k) * ch : (j + k + 1) * ch, k * ch : (k + 1) * ch] = mixed[i]
    for i in range(4):
        for k in range(2):
            at = 3 * (1 - k)
            big2[i, at * ch : (at + 1) * ch, k * ch : (k + 1) * ch] = jnp.zeros((ch, ch), BF16)

    for d in range(1, na):
        key_copy(d).wait()
    table = everyone[...].reshape(na * here, ch)
    pick = (lax.broadcasted_iota(jnp.int32, (agents, agents), 0) == slot[...]).astype(F32).astype(BF16)
    keys = lax.dot_general(
        table, pick, (((0,), (0,)), ((), ())), preferred_element_type=F32
    ).astype(BF16)
    keys_out[...] = keys

    bias1 = jnp.concatenate([b1[...], b1[...]], axis=1)
    bias2 = jnp.concatenate([b2[...], b2[...]], axis=1)

    def layer_one(u):
        s, g = u // 2, u % 2

        def unpack():
            for t in range(0, pairs // 2 + 4, 4):
                at = pl.ds(g * (pairs // 2) + t, 4)
                for par in range(2):
                    for side, col in ((0, PAD - 4), (1, PAD + cols)):
                        xp1[s, at, par, col : col + 4, :] = (
                            p_land[s, side, at, 4 * par : 4 * par + 4, :]
                        )

        def body():
            def piece(i, j):
                parts = [
                    xp1[
                        s, pl.ds(g * half // 2 + 4 * h + 2 * i, 2), :,
                        PAD - 4 + 4 * j : PAD - 4 + 4 * j + cols, :,
                    ].reshape(4 * cols, ch)
                    for h in range(half // 8)
                ]
                return jnp.concatenate(parts, axis=0)

            lhs = jnp.concatenate([piece(i, j) for i in range(4) for j in range(3)], axis=1)
            out = jnp.dot(lhs, big1[...], preferred_element_type=F32)
            out = jnp.maximum(out + bias1, 0.0).astype(BF16)
            for h in range(half // 8):
                for o in range(2):
                    y = out[h * 4 * cols : (h + 1) * 4 * cols, o * ch : (o + 1) * ch]
                    y = y.reshape(4, groups, 2, 8, ch)
                    at = pl.ds(8 + half * g + 8 * h + 4 * o, 4)
                    q2[s, at, flat : flat + groups] = y[:, :, 0]
                    q2[s, at, 1 : 1 + groups] = y[:, :, 1]

        @pl.when(g == 0)
        def _():
            recv_halo(0, s, (1, 2, 3, 6, 7))

        @pl.when(g == 1)
        def _():
            recv_halo(0, s, (0, 4, 5, 8, 9))

        unpack()
        body()

        @pl.when(g == 0)
        def _():
            start_halo(1, s, (4, 5, 0, 3, 2))

        @pl.when(g == 1)
        def _():
            start_halo(1, s, (6, 7, 1, 9, 8, 11, 10))

    size = half * cols
    share = size // SHARES
    blocks = rows // BLOCK

    spare = scenes * blocks

    def fold(u, p):
        at = (u * half + p * (half // SHARES)) // BLOCK
        if not isinstance(u, int):
            at = jnp.where(u >= 0, at, spare)
        top, total = tops[at], sums[at]
        step = 64
        new = jnp.maximum(top, highs[p])
        total = total * jnp.exp(top - new)
        for k in range(share // step):
            low = p * share + k * step
            part = z_ref[low : low + step].reshape(step // 8, 8, agents)
            total = total + jnp.sum(jnp.exp(part - new[None]), axis=0)
        tops[at] = new
        sums[at] = total

    def layer_two(u):
        s, g = u // 2, u % 2

        @pl.when(g == 0)
        def _():
            recv_halo(1, s, (1, 2, 3, 6, 7, 8, 9))

        @pl.when(g == 1)
        def _():
            recv_halo(1, s, (0, 4, 5, 10, 11))

        def lhs(i):
            first, second, sign = TAPS[i]
            across = []
            for j in range(4):
                at = (j % 2) * flat + j // 2
                down = []
                for h in range(half // 16):
                    row = half * g + 16 * h
                    x = q2[s, pl.ds(row + 8 * first, 8), at : at + groups]
                    y = q2[s, pl.ds(row + 8 * second, 8), at : at + groups]
                    down.append((x + y if sign > 0 else x - y).reshape(8 * groups * 8, ch))
                across.append(jnp.concatenate(down, axis=0))
            return jnp.concatenate(across, axis=1)

        m = []
        for i in range(4):
            m.append(jnp.dot(lhs(i), big2[i], preferred_element_type=F32))
            for p in range(i * SHARES // 4, (i + 1) * SHARES // 4):
                fold(u - 1, p)
        outs = (
            jnp.maximum(m[0] + (m[1] + m[2]) + bias2, 0.0).astype(BF16),
            jnp.maximum((m[1] - m[2]) - m[3] + bias2, 0.0).astype(BF16),
        )
        for h in range(half // 16):
            for o in range(2):
                for k in range(2):
                    y = outs[o][h * 64 * groups : (h + 1) * 64 * groups, k * ch : (k + 1) * ch]
                    at = s * rows + half * g + 16 * h + 8 * o
                    l2[pl.ds(at, 8), :, k] = y.reshape(8, groups, 8, ch)
        for p in range(SHARES):
            deep = half // SHARES
            at = s * rows + half * g + p * deep
            y = l2[pl.ds(at, deep)].reshape(share, ch)
            z = jnp.dot(y, keys_out[...], preferred_element_type=F32)
            z_ref[p * share : (p + 1) * share] = z
            highs[p] = jnp.max(z.reshape(share // 8, 8, agents), axis=0)

        @pl.when(g == 1)
        def _():
            out_copy(s).start()

    def settle(s):
        peak = jnp.full((1, agents), NEG, F32)
        mass = jnp.zeros((1, agents), F32)
        for block in range(blocks):
            top = tops[s * blocks + block]
            total = sums[s * blocks + block]
            high = jnp.max(top, axis=0, keepdims=True)
            part = jnp.sum(total * jnp.exp(top - high), axis=0, keepdims=True)
            block_row = r * blocks + block
            block_col = q * cols // BLOCK
            ok = (
                (regions[0:1] <= block_row) & (block_row < regions[1:2])
                & (regions[2:3] <= block_col) & (block_col < regions[3:4])
            )
            high = jnp.where(ok, high, NEG)
            part = jnp.where(ok, part, 0.0)
            new = jnp.maximum(peak, high)
            mass = mass * jnp.exp(peak - new) + part * jnp.exp(high - new)
            peak = new
        stats[0, 0, s : s + 1] = peak
        stats[0, 1, s : s + 1] = mass

    def stat_copy(d, rr, qq):
        return pltpu.make_async_remote_copy(
            src_ref=stats.at[0], dst_ref=stats.at[d],
            send_sem=s_send.at[d], recv_sem=s_recv.at[d],
            device_id=place(rr, qq), device_id_type=MESH,
        )

    def out_copy(s):
        return pltpu.make_async_copy(l2.at[pl.ds(s * rows, rows)], l2_out.at[s], out_sem.at[s])

    pl.loop(0, 2 * scenes)(layer_one)
    pl.loop(0, 2 * scenes)(layer_two)
    for p in range(SHARES):
        fold(2 * scenes - 1, p)
    for s in range(scenes):
        settle(s)
    others(lambda *to: stat_copy(*to).start())
    for phase in range(2):
        for s in range(scenes):
            sent_halo(phase, s)
    others(lambda *to: stat_copy(*to).wait_recv())
    peaks, parts = stats[:, 0], stats[:, 1]
    top = jnp.max(peaks, axis=0)
    part = jnp.sum(parts * jnp.exp(peaks - top[None]), axis=0)
    norm_out[...] = top + jnp.log(part)
    others(lambda *to: stat_copy(*to).wait_send())
    for s in range(scenes):
        out_copy(s).wait()


def heat_kernel(field, keys, norm, out, cells, heat, in_sem, out_sem):
    scenes, total, _ = field.shape
    slots, size = heat.shape[0], heat.shape[1]
    batch = cells.shape[1]
    parts = scenes * total // size
    per = total // size
    many = batch // size

    def load(t):
        return pltpu.make_async_copy(
            field.at[t * batch // total, pl.ds(t * batch % total, batch)], cells.at[t], in_sem.at[t]
        )

    def store(t):
        return pltpu.make_async_copy(
            heat.at[t % slots], out.at[t // per, pl.ds(t % per * size, size)], out_sem.at[t % slots]
        )

    for t in range(cells.shape[0]):
        load(t).start()

    @pl.loop(0, parts)
    def _(t):
        @pl.when(t % many == 0)
        def _():
            load(t // many).wait()

        @pl.when(t >= slots)
        def _():
            store(t - slots).wait()

        y = cells[t // many, pl.ds(t % many * size, size)]
        z = jnp.dot(y, keys[...], preferred_element_type=F32)
        heat[t % slots] = z - norm[pl.ds(t // per, 1)]
        store(t).start()

    for t in range(parts - slots, parts):
        store(t).wait()


def shards(nr, nc, na, raster, w1, b1, w2, b2, queries, slot, regions):
    scenes, rows, cols, ch = raster.shape
    agents = slot.shape[0]
    nq = nc * na
    vmem = pl.BlockSpec(memory_space=pltpu.VMEM)
    anywhere = pl.BlockSpec(memory_space=pl.ANY)
    dma = pltpu.SemaphoreType.DMA
    field, keys, norm = pl.pallas_call(
        functools.partial(field_kernel, nr, nc, na, scenes, rows, cols, agents),
        out_shape=(
            jax.ShapeDtypeStruct((scenes, rows, cols // 16, 2, 8, ch), BF16),
            jax.ShapeDtypeStruct((ch, agents), BF16),
            jax.ShapeDtypeStruct((scenes, agents), F32),
        ),
        in_specs=[anywhere, anywhere, vmem, anywhere, vmem, vmem, vmem, vmem],
        out_specs=(anywhere, vmem, vmem),
        scratch_shapes=[
            pltpu.VMEM((scenes, rows // 2 + 4, 2, cols + 2 * PAD, ch), BF16),
            pltpu.VMEM((scenes, rows + 16, 2 * (cols // 16 + 1), 8, ch), BF16),
            pltpu.VMEM((scenes * rows, cols // 16, 2, 8, ch), BF16),
            pltpu.VMEM((rows // 2 * cols, agents), F32),
            pltpu.VMEM((scenes * (rows // BLOCK) + 1, 8, agents), F32),
            pltpu.VMEM((scenes * (rows // BLOCK) + 1, 8, agents), F32),
            pltpu.VMEM((SHARES, 8, agents), F32),
            pltpu.VMEM((scenes, 2, rows // 2, 8, ch), BF16),
            pltpu.VMEM((scenes, 2, rows // 2 + 4, 8, ch), BF16),
            pltpu.VMEM((12 * ch, 2 * ch), BF16),
            pltpu.VMEM((4, 4 * ch, 2 * ch), BF16),
            pltpu.VMEM((na,) + queries.shape, BF16),
            pltpu.VMEM((nr * nq, 2, scenes, agents), F32),
            pltpu.VMEM(w1.shape, BF16),
            pltpu.VMEM(w2.shape, BF16),
            dma((scenes,)),
            dma((2,)),
            dma((scenes,)),
            dma((2, scenes, 12)),
            dma((2, scenes, 12)),
            dma((na,)),
            dma((na,)),
            dma((nr * nq,)),
            dma((nr * nq,)),
        ],
        compiler_params=pltpu.CompilerParams(
            collective_id=0, has_side_effects=True, vmem_limit_bytes=60 * 1024 * 1024
        ),
        name="field",
    )(
        raster.reshape(scenes, rows // 2, 2, cols, ch), w1, b1.reshape(1, -1), w2, b2.reshape(1, -1),
        queries, slot.reshape(1, -1), regions.T,
    )
    cells = rows * cols
    size = min(1024, cells)
    batch = min(2048, cells)
    parts = scenes * cells // size
    slots = min(8, parts)
    heat = pl.pallas_call(
        heat_kernel,
        out_shape=jax.ShapeDtypeStruct((scenes, cells, agents), F32),
        in_specs=[anywhere, vmem, vmem],
        out_specs=anywhere,
        scratch_shapes=[
            pltpu.VMEM((scenes * cells // batch, batch, ch), BF16),
            pltpu.VMEM((slots, size, agents), F32),
            dma((scenes * cells // batch,)),
            dma((slots,)),
        ],
        name="heat",
    )(field.reshape(scenes, cells, ch), keys, norm)
    return heat.reshape(scenes, rows, cols, agents)


def solution(mesh):
    in_specs = (P(None, "row", ("col", "agent"), None), P(), P(), P(), P(), P("agent", None), P(), P())
    out_specs = P(None, "row", ("col", "agent"), None)
    sizes = (mesh.shape["row"], mesh.shape["col"], mesh.shape["agent"])
    return jax.shard_map(
        functools.partial(shards, *sizes), mesh=mesh, in_specs=in_specs, out_specs=out_specs, check_vma=False
    )
```
